32 devices in a mesh: nodes: 8 (over y, x, core), heads: 4 (over z).
Axes of the slice: x: 2, y: 2, z: 4, core: 2. Of those that a mesh axis runs over, the one named last changes fastest.
Arguments:
- grid_state: bfloat16 [8192, 1024], P('nodes', 'heads'), may hold values from -6 to 6
- mesh_state: bfloat16 [2048, 1024], P('nodes', 'heads'), may hold values from -6 to 6
- encoder_query: bfloat16 [1024, 512], P('nodes', 'heads'), may hold values from -0.1875 to 0.1875
- encoder_key: bfloat16 [1024, 512], P('nodes', 'heads'), may hold values from -0.1875 to 0.1875
- encoder_value: bfloat16 [1024, 512], P('nodes', 'heads'), may hold values from -0.1875 to 0.1875
- encoder_output: bfloat16 [512, 1024], P('heads', 'nodes'), may hold values from -0.25 to 0.25
- window_query: bfloat16 [1024, 512], P('nodes', 'heads'), may hold values from -0.1875 to 0.1875
- window_key: bfloat16 [1024, 512], P('nodes', 'heads'), may hold values from -0.1875 to 0.1875
- window_value: bfloat16 [1024, 512], P('nodes', 'heads'), may hold values from -0.1875 to 0.1875
- window_output: bfloat16 [512, 1024], P('heads', 'nodes'), may hold values from -0.25 to 0.25
- expand_weight: bfloat16 [1024, 2048], P('nodes', 'heads'), may hold values from -0.1875 to 0.1875
- shrink_weight: bfloat16 [2048, 1024], P('heads', 'nodes'), may hold values from -0.125 to 0.125
- decoder_query: bfloat16 [1024, 512], P('nodes', 'heads'), may hold values from -0.1875 to 0.1875
- decoder_key: bfloat16 [1024, 512], P('nodes', 'heads'), may hold values from -0.1875 to 0.1875
- decoder_value: bfloat16 [1024, 512], P('nodes', 'heads'), may hold values from -0.1875 to 0.1875
- decoder_output: bfloat16 [512, 1024], P('heads', 'nodes'), may hold values from -0.25 to 0.25
- encoder_blocks: int32 [16, 8], P('nodes'), may hold values from 0 to 63, as said below
- encoder_count: int32 [16], P('nodes'), may hold values from 2 to 8, as said below
- window_offsets: int32 [16, 4], P('nodes'), may hold values from -2 to 2, as said below
- decoder_blocks: int32 [64, 3], P('nodes'), may hold values from 0 to 15, as said below
- decoder_count: int32 [64], P('nodes'), may hold values from 1 to 3, as said below
Outputs:
- grid_out: bfloat16 [8192, 1024], P('nodes', 'heads')
- mesh_out: bfloat16 [2048, 1024], P('nodes', 'heads')
The draws below stay inside these ranges and needn't reach their ends.
Inputs may be any that keep to these rules, and one draw needn't show every extreme that they name: `encoder_blocks`: row m names 8 different grid blocks; each lies among the grid blocks of the index of nodes that holds mesh block m, or in the nearer half of the grid blocks of the index on either side. The first encoder_count[m] slots of row m are live; every mesh block held by the first or last eighth of the indices of nodes has all 8 slots live. `window_offsets`: each row holds 4 different offsets, the first of them 0. `decoder_blocks`: row g names 3 different mesh blocks; each lies among the mesh blocks of the index of nodes that holds grid block g, or is the one block next to them on either side. The first decoder_count[g] slots of row g are live; every grid block of the first index of nodes has all 3 slots live.
All inputs are finite; a program needn't handle non-finite values.
Results may differ from the reference program's by a relative error of at most 0.012.
Values may be sent and summed in bfloat16 or wider, within the bound.
A program may use at most 64 MiB of HBM per device.

```python
import jax
import jax.numpy as jnp
from jax import lax

D = 1024
HEADS = 8
HEAD_DIM = 64
FF = 2048
TILE = 128
ENC_SLOTS = 8
DEC_SLOTS = 3
WIN = 4
REACH = 2
GRID_DEV = 1024
MESH_DEV = 256
GRID = 8192
MESH = 2048


def distinct_pick(subkey, candidates, in_range, needed):
    column_count = candidates.shape[1]
    column_index = jnp.arange(column_count, dtype=jnp.int32)[None, :]
    random_part = jax.random.randint(subkey, candidates.shape, 0, 1 << 20)
    ranking = random_part * column_count + column_index
    ranking = jnp.where(in_range, ranking, -1 - column_index)
    _, chosen = lax.top_k(ranking, needed)
    return jnp.take_along_axis(candidates, chosen, axis=1).astype(jnp.int32)


def draw_encoder_blocks(key, part):
    grid_tiles = GRID_DEV // TILE
    mesh_tiles = MESH_DEV // TILE
    owner_index = jnp.arange(MESH // TILE, dtype=jnp.int32) // mesh_tiles
    first_tile = owner_index * grid_tiles - grid_tiles // 2
    candidates = first_tile[:, None] + jnp.arange(2 * grid_tiles, dtype=jnp.int32)[None, :]
    in_range = (candidates >= 0) & (candidates < GRID // TILE)
    return distinct_pick(jax.random.fold_in(key, 11), candidates, in_range, ENC_SLOTS)


def draw_encoder_count(key, part):
    devices = MESH // MESH_DEV
    owner_index = jnp.arange(MESH // TILE, dtype=jnp.int32) // (MESH_DEV // TILE)
    live_count = jax.random.randint(jax.random.fold_in(key, 12), (MESH // TILE,), 2, ENC_SLOTS + 1)
    crowded = (owner_index * 8 < devices) | (owner_index * 8 >= 7 * devices)
    return jnp.where(crowded, ENC_SLOTS, live_count).astype(jnp.int32)


def draw_window_offsets(key, part):
    tile_count = MESH // TILE
    others = jnp.concatenate([jnp.arange(-REACH, 0, dtype=jnp.int32), jnp.arange(1, REACH + 1, dtype=jnp.int32)])
    candidates = jnp.broadcast_to(others[None, :], (tile_count, 2 * REACH))
    in_range = jnp.ones((tile_count, 2 * REACH), dtype=bool)
    picked = distinct_pick(jax.random.fold_in(key, 13), candidates, in_range, WIN - 1)
    return jnp.concatenate([jnp.zeros((tile_count, 1), jnp.int32), picked], axis=1)


def draw_decoder_blocks(key, part):
    grid_tiles = GRID_DEV // TILE
    mesh_tiles = MESH_DEV // TILE
    owner_index = jnp.arange(GRID // TILE, dtype=jnp.int32) // grid_tiles
    first_tile = owner_index * mesh_tiles - 1
    candidates = first_tile[:, None] + jnp.arange(mesh_tiles + 2, dtype=jnp.int32)[None, :]
    in_range = (candidates >= 0) & (candidates < MESH // TILE)
    return distinct_pick(jax.random.fold_in(key, 14), candidates, in_range, DEC_SLOTS)


def draw_decoder_count(key, part):
    owner_index = jnp.arange(GRID // TILE, dtype=jnp.int32) // (GRID_DEV // TILE)
    live_count = jax.random.randint(jax.random.fold_in(key, 15), (GRID // TILE,), 1, DEC_SLOTS + 1)
    return jnp.where(owner_index == 0, DEC_SLOTS, live_count).astype(jnp.int32)


def level_of(own_key, shape, pieces, least, largest):
    factor_of, own = 1.0, jax.random.fold_in(own_key, 6)
    for position, parts in pieces:
        heights = jnp.exp(jax.random.uniform(jax.random.fold_in(own, position), (parts,), jnp.float32, least / len(pieces), largest / len(pieces)))
        factor_of = factor_of * jnp.repeat(heights, shape[position] // parts).reshape([-1 if axis == position else 1 for axis in range(len(shape))])
    return factor_of


def scatter_about(key, dims, width, limit, cuts=(), kind=jnp.bfloat16):
    result = width * jax.random.normal(key, dims, jnp.float32)
    if cuts:
        result = result * level_of(key, dims, cuts, -0.22, 0.18)
    return jnp.clip(result, -limit, limit).astype(kind)


def setup_inputs(seed: int = 0) -> dict:
    seeds = jax.random.split(jax.random.key(seed), 22)
    grid_state = scatter_about(seeds[0], (GRID, D), 1.0, 6.0, ((0, 8), (1, 4)))
    mesh_state = scatter_about(seeds[1], (MESH, D), 1.0, 6.0, ((0, 8), (1, 4)))
    encoder_query = scatter_about(seeds[2], (D, HEADS * HEAD_DIM), D ** -0.5, 0.1875, ((0, 8), (1, 4)))
    encoder_key = scatter_about(seeds[3], (D, HEADS * HEAD_DIM), D ** -0.5, 0.1875, ((0, 8), (1, 4)))
    encoder_value = scatter_about(seeds[4], (D, HEADS * HEAD_DIM), D ** -0.5, 0.1875, ((0, 8), (1, 4)))
    encoder_output = scatter_about(seeds[5], (HEADS * HEAD_DIM, D), (HEADS * HEAD_DIM) ** -0.5, 0.25, ((0, 4), (1, 8)))
    window_query = scatter_about(seeds[6], (D, HEADS * HEAD_DIM), D ** -0.5, 0.1875, ((0, 8), (1, 4)))
    window_key = scatter_about(seeds[7], (D, HEADS * HEAD_DIM), D ** -0.5, 0.1875, ((0, 8), (1, 4)))
    window_value = scatter_about(seeds[8], (D, HEADS * HEAD_DIM), D ** -0.5, 0.1875, ((0, 8), (1, 4)))
    window_output = scatter_about(seeds[9], (HEADS * HEAD_DIM, D), (HEADS * HEAD_DIM) ** -0.5, 0.25, ((0, 4), (1, 8)))
    expand_weight = scatter_about(seeds[10], (D, FF), D ** -0.5, 0.1875, ((0, 8), (1, 4)))
    shrink_weight = scatter_about(seeds[11], (FF, D), FF ** -0.5, 0.125, ((0, 4), (1, 8)))
    decoder_query = scatter_about(seeds[12], (D, HEADS * HEAD_DIM), D ** -0.5, 0.1875, ((0, 8), (1, 4)))
    decoder_key = scatter_about(seeds[13], (D, HEADS * HEAD_DIM), D ** -0.5, 0.1875, ((0, 8), (1, 4)))
    decoder_value = scatter_about(seeds[14], (D, HEADS * HEAD_DIM), D ** -0.5, 0.1875, ((0, 8), (1, 4)))
    decoder_output = scatter_about(seeds[15], (HEADS * HEAD_DIM, D), (HEADS * HEAD_DIM) ** -0.5, 0.25, ((0, 4), (1, 8)))
    encoder_blocks = draw_encoder_blocks(jax.random.fold_in(seeds[21], 71), 0)
    encoder_count = draw_encoder_count(jax.random.fold_in(seeds[21], 71), 0)
    window_offsets = draw_window_offsets(jax.random.fold_in(seeds[21], 71), 0)
    decoder_blocks = draw_decoder_blocks(jax.random.fold_in(seeds[21], 71), 0)
    decoder_count = draw_decoder_count(jax.random.fold_in(seeds[21], 71), 0)
    return {"grid_state": grid_state, "mesh_state": mesh_state, "encoder_query": encoder_query, "encoder_key": encoder_key, "encoder_value": encoder_value, "encoder_output": encoder_output, "window_query": window_query, "window_key": window_key, "window_value": window_value, "window_output": window_output, "expand_weight": expand_weight, "shrink_weight": shrink_weight, "decoder_query": decoder_query, "decoder_key": decoder_key, "decoder_value": decoder_value, "decoder_output": decoder_output, "encoder_blocks": encoder_blocks, "encoder_count": encoder_count, "window_offsets": window_offsets, "decoder_blocks": decoder_blocks, "decoder_count": decoder_count}


EPSILON = 1e-05

def normalize(values):
    values = values.astype(jnp.float32)
    average = lax.optimization_barrier(jnp.mean(values, axis=-1, keepdims=True))
    centred = values - average
    spread = lax.optimization_barrier(jnp.mean(centred * centred, axis=-1, keepdims=True))
    return (centred * lax.rsqrt(spread + EPSILON)).astype(jnp.bfloat16)

def project(source, weight, scaling):
    return (jnp.dot(source, weight, preferred_element_type=jnp.float32) * scaling).astype(jnp.bfloat16)

def residual(base, mixture, weight):
    update = jnp.dot(mixture, weight, preferred_element_type=jnp.float32)
    return (base.astype(jnp.float32) + update).astype(jnp.bfloat16)

def attend(queries, key_rows, value_rows, key_mask):
    head_count = queries.shape[1] // HEAD_DIM
    split_query = queries.astype(jnp.float32).reshape(queries.shape[0], head_count, HEAD_DIM)
    split_key = key_rows.astype(jnp.float32).reshape(key_rows.shape[0], head_count, HEAD_DIM)
    split_value = value_rows.astype(jnp.float32).reshape(value_rows.shape[0], head_count, HEAD_DIM)
    scores = jnp.einsum('qhd,khd->hqk', split_query, split_key)
    scores = jnp.where(key_mask[None, None, :], scores, -1e+30)
    highest = lax.optimization_barrier(jnp.max(scores, axis=-1, keepdims=True))
    weights = jnp.exp(scores - highest)
    weights = (weights / lax.optimization_barrier(jnp.sum(weights, axis=-1, keepdims=True))).astype(jnp.bfloat16)
    weights = lax.optimization_barrier(weights).astype(jnp.float32)
    mixture = jnp.einsum('hqk,khd->qhd', weights, split_value)
    return mixture.reshape(queries.shape).astype(jnp.bfloat16)

def reference(grid_state, mesh_state, encoder_query, encoder_key, encoder_value, encoder_output, window_query, window_key, window_value, window_output, expand_weight, shrink_weight, decoder_query, decoder_key, decoder_value, decoder_output, encoder_blocks, encoder_count, window_offsets, decoder_blocks, decoder_count):
    scaling = HEAD_DIM ** (-0.5)
    features = HEADS * HEAD_DIM
    grid_tiles = GRID // TILE
    mesh_tiles = MESH // TILE
    grid_norm = normalize(grid_state)
    grid_keys = project(grid_norm, encoder_key, 1.0).reshape(grid_tiles, TILE, features)
    grid_values = project(grid_norm, encoder_value, 1.0).reshape(grid_tiles, TILE, features)
    grid_queries = project(grid_norm, decoder_query, scaling)
    mesh_queries = project(normalize(mesh_state), encoder_query, scaling)
    enc_slots = jnp.arange(ENC_SLOTS, dtype=jnp.int32)

    def encode(arguments):
        queries, chosen, live_count = arguments
        key_mask = jnp.repeat(enc_slots < live_count, TILE)
        key_rows = grid_keys[chosen].reshape(ENC_SLOTS * TILE, features)
        value_rows = grid_values[chosen].reshape(ENC_SLOTS * TILE, features)
        return attend(queries, key_rows, value_rows, key_mask)
    encoded = lax.map(encode, (mesh_queries.reshape(mesh_tiles, TILE, features), encoder_blocks, encoder_count))
    mesh_one = residual(mesh_state, encoded.reshape(MESH, features), encoder_output)
    norm_one = normalize(mesh_one)
    window_queries = project(norm_one, window_query, scaling)
    window_keys = project(norm_one, window_key, 1.0).reshape(mesh_tiles, TILE, features)
    window_values = project(norm_one, window_value, 1.0).reshape(mesh_tiles, TILE, features)

    def window(arguments):
        queries, tile_index, offsets = arguments
        reached = tile_index + offsets
        key_mask = jnp.repeat((reached >= 0) & (reached < mesh_tiles), TILE)
        chosen = jnp.clip(reached, 0, mesh_tiles - 1)
        key_rows = window_keys[chosen].reshape(WIN * TILE, features)
        value_rows = window_values[chosen].reshape(WIN * TILE, features)
        return attend(queries, key_rows, value_rows, key_mask)
    tile_numbers = jnp.arange(mesh_tiles, dtype=jnp.int32)
    windowed = lax.map(window, (window_queries.reshape(mesh_tiles, TILE, features), tile_numbers, window_offsets))
    mesh_two = residual(mesh_one, windowed.reshape(MESH, features), window_output)
    hidden = jax.nn.gelu(jnp.dot(normalize(mesh_two), expand_weight, preferred_element_type=jnp.float32), approximate=False).astype(jnp.bfloat16)
    mesh_three = residual(mesh_two, hidden, shrink_weight)
    norm_three = normalize(mesh_three)
    mesh_keys = project(norm_three, decoder_key, 1.0).reshape(mesh_tiles, TILE, features)
    mesh_values = project(norm_three, decoder_value, 1.0).reshape(mesh_tiles, TILE, features)
    dec_slots = jnp.arange(DEC_SLOTS, dtype=jnp.int32)

    def decode(arguments):
        queries, chosen, live_count = arguments
        key_mask = jnp.repeat(dec_slots < live_count, TILE)
        key_rows = mesh_keys[chosen].reshape(DEC_SLOTS * TILE, features)
        value_rows = mesh_values[chosen].reshape(DEC_SLOTS * TILE, features)
        return attend(queries, key_rows, value_rows, key_mask)
    decoded = lax.map(decode, (grid_queries.reshape(grid_tiles, TILE, features), decoder_blocks, decoder_count))
    grid_out = residual(grid_state, decoded.reshape(GRID, features), decoder_output)
    return (grid_out, mesh_three)
```

```python
import functools

import jax
import jax.numpy as jnp
from jax import lax
from jax.experimental import pallas as pl
from jax.experimental.pallas import tpu as pltpu
from jax.sharding import PartitionSpec as P

HEAD_DIM = 64
TILE = 128
EPSILON = 1e-05
PARTS = 4
MESH = pl.DeviceIdType.MESH
F32 = jnp.float32
BF16 = jnp.bfloat16


def normalize(values):
    average = jnp.mean(values, axis=-1, keepdims=True)
    centred = values - average
    spread = jnp.mean(centred * centred, axis=-1, keepdims=True)
    return (centred * lax.rsqrt(spread + EPSILON)).astype(BF16)


def dot(a, b):
    return jnp.dot(a, b, preferred_element_type=F32)


def dot_t(a, b):
    return lax.dot_general(a, b, (((1,), (1,)), ((), ())), preferred_element_type=F32)


def attend(query, key, value, mask):
    columns = query.shape[1]
    heads = columns // HEAD_DIM
    lane = lax.broadcasted_iota(jnp.int32, (1, columns), 1) // HEAD_DIM
    query = query.astype(F32)
    stacked = jnp.concatenate(
        [jnp.where(lane == i, query, 0.0) for i in range(heads)], axis=0
    ).astype(BF16)
    scores = dot_t(stacked, key)
    scores = jnp.where(mask, scores, -1e30)
    weights = jnp.exp(scores - jnp.max(scores, axis=-1, keepdims=True))
    weights = (weights * (1.0 / jnp.sum(weights, axis=-1, keepdims=True))).astype(BF16)
    mixed = dot(weights, value)
    rows = query.shape[0]
    result = mixed[:rows]
    for i in range(1, heads):
        result = jnp.where(lane == i, mixed[i * rows : (i + 1) * rows], result)
    return result.astype(BF16)


def kernel(count, lanes, gathers, *refs):
    N, H = count, lanes
    (eb, ec, wo, db, dc, grid_in, mesh_in) = refs[:7]
    refs = refs[7:]
    if gathers:
        a_in, b_in, c_in = refs[:3]
        grid_out, mesh_out = refs[3:5]
        refs = refs[5:]
        a_buf, b_buf, c_own, c_buf = refs[:4]
        refs = refs[4:]
    else:
        a_buf, b_buf, c_buf = refs[:3]
        grid_out, mesh_out = refs[3:5]
        refs = refs[5:]
    (
        grid_buf, kv, gq, mesh_buf, enc_buf, win_buf, two_buf, wkv, rs_src, rs_dst,
        three_buf, dkv, dec_buf, zs, zr, hs, hr, rs_s, rs_r,
    ) = refs[:19]
    if gathers:
        ns, nf, nr = refs[19:]
    scaling = HEAD_DIM ** (-0.5)
    n = lax.axis_index("nodes")
    h = lax.axis_index("heads")
    grid_rows, part_features = grid_in.shape
    mesh_rows = mesh_in.shape[0]
    chunk = grid_rows // PARTS
    rim = grid_rows // 2
    grid_tiles, mesh_tiles = grid_rows // TILE, mesh_rows // TILE
    cols = gq.shape[1]

    barrier = pltpu.get_barrier_semaphore()

    def greet(node, lane):
        pl.semaphore_signal(barrier, inc=1, device_id=(node, lane), device_id_type=MESH)

    node_steps = range(1, N) if gathers else (1, N - 1)
    for d in node_steps:
        greet(lax.rem(n + d, N), h)
    for d in range(1, H):
        greet(n, lax.rem(h + d, H))
    pl.semaphore_wait(barrier, len(node_steps) + H - 1)

    def copy(src, dst, send, recv, device):
        return pltpu.make_async_remote_copy(
            src_ref=src, dst_ref=dst, send_sem=send, recv_sem=recv,
            device_id=device, device_id_type=MESH,
        )

    def link(item, src, dst, slot, way):
        lane = h + 1 if way == 0 else h - 1
        return copy(src, dst, zs.at[way, item, slot], zr.at[item, slot], (n, lane))

    def chain_start(item, view, src=None):
        src = view(h) if src is None else src

        @pl.when(h + 1 < H)
        def _():
            link(item, src, view(h), h, 0).start()

        @pl.when(h > 0)
        def _():
            link(item, src, view(h), h, 1).start()

    def chain_step(item, view, s):
        @pl.when(h >= s)
        def _():
            a = h - s
            link(item, view(a), view(a), a, 1).wait_recv()

            @pl.when(h + 1 < H)
            def _():
                link(item, view(a), view(a), a, 0).start()

        @pl.when(h + s < H)
        def _():
            b = h + s
            link(item, view(b), view(b), b, 0).wait_recv()

            @pl.when(h > 0)
            def _():
                link(item, view(b), view(b), b, 1).start()

    def chain_drain(item, view):
        for s in range(H):

            @pl.when((h >= s) & (h + 1 < H))
            def _():
                link(item, view(h - s), view(h - s), h - s, 0).wait_send()

            @pl.when((h + s < H) & (h > 0))
            def _():
                link(item, view(h + s), view(h + s), h + s, 1).wait_send()

    beside = n + 1 - 2 * lax.rem(n, 2)

    def gather_start(item, view, src):
        for j in range(1, N // 2):
            peer = lax.rem(n + 2 * j, N)
            copy(src, view(n), ns.at[item, j], nr.at[item, n], (peer, h)).start()
        copy(src, view(n), nf.at[item, n], nr.at[item, n], (beside, h)).start()
        view(n)[...] = src[...]

    def gather_pass(item, view):
        for j in range(1, N // 2):
            m = lax.rem(n + N - 2 * j, N)
            forward = copy(view(m), view(m), nf.at[item, m], nr.at[item, m], (beside, h))
            forward.wait_recv()
            forward.start()

    def gather_wait(item, view):
        for j in range(N // 2):
            m = lax.rem(beside + N - 2 * j, N)
            copy(view(m), view(m), nf.at[item, m], nr.at[item, m], (beside, h)).wait_recv()

    def gather_drain(item, view):
        for j in range(N // 2):
            if j:
                copy(view(n), view(n), ns.at[item, j], nr.at[item, n], (beside, h)).wait_send()
            m = lax.rem(n + N - 2 * j, N)
            copy(view(m), view(m), nf.at[item, m], nr.at[item, m], (beside, h)).wait_send()

    def rows_of(buf, size):
        return lambda m: buf.at[pl.ds(pl.multiple_of(m * size, size), size), :]

    def grid_view(c):
        return lambda s: grid_buf.at[s, pl.ds(c * chunk, chunk), :]

    def dec_view(c):
        return lambda s: dec_buf.at[s, pl.ds(c * chunk, chunk), :]

    whole = lambda buf: (lambda s: buf.at[s])
    MESH_ITEM, OUT_ITEM, ENC_ITEM, WIN_ITEM, THREE_ITEM = range(PARTS, PARTS + 5)
    DEC_ITEM = PARTS + 5

    def halo(way, k, src, dst):
        node = n - 1 if way == 0 else n + 1
        return copy(src, dst, hs.at[way, k], hr.at[way, k], (node, h))

    def halo_ok(way):
        return n > 0 if way == 0 else n + 1 < N

    if gathers:
        shard = a_in.shape[0]
        a_view, b_view = rows_of(a_buf, shard), rows_of(b_buf, shard)
        c_view = lambda s: (
            lambda m: c_buf.at[s, pl.ds(pl.multiple_of(m * shard, shard), shard), :]
        )
        gather_start(0, a_view, a_in)
    for c in range(PARTS):
        chain_start(c, grid_view(c), grid_in.at[pl.ds(c * chunk, chunk), :])
    chain_start(MESH_ITEM, whole(mesh_buf), mesh_in)
    if gathers:
        gather_start(1, b_view, b_in)
        chain_start(OUT_ITEM, whole(c_own), c_in)
        c_own[h] = c_in[...]
    grid_buf[h] = grid_in[...]
    mesh_buf[h] = mesh_in[...]

    @pl.when(n == 0)
    def _():
        kv[0:rim, :] = jnp.zeros((rim, 2 * cols), BF16)
        wkv[0:mesh_rows, :] = jnp.zeros((mesh_rows, 2 * cols), BF16)
        dkv[0:TILE, :] = jnp.zeros((TILE, 2 * cols), BF16)

    @pl.when(n == N - 1)
    def _():
        kv[rim + grid_rows :, :] = jnp.zeros((rim, 2 * cols), BF16)
        wkv[2 * mesh_rows :, :] = jnp.zeros((mesh_rows, 2 * cols), BF16)
        dkv[TILE + mesh_rows :, :] = jnp.zeros((TILE, 2 * cols), BF16)

    for s in range(1, H):
        for c in range(PARTS):
            if s == 1 and c == 1 and gathers:
                gather_pass(0, a_view)
            if s < H - 1:
                chain_step(c, grid_view(c), s)
        if s < H - 1:
            chain_step(MESH_ITEM, whole(mesh_buf), s)
            if gathers:
                chain_step(OUT_ITEM, whole(c_own), s)
    if gathers:
        gather_wait(0, a_view)

    rim_parts = PARTS // 2

    def halo_enc(c):
        here = kv.at[pl.ds(rim + c * chunk, chunk), :]
        if c < rim_parts:
            return 0, c, here, kv.at[pl.ds(rim + grid_rows + c * chunk, chunk), :]
        k = c - rim_parts
        return 1, k, here, kv.at[pl.ds(k * chunk, chunk), :]

    def start_halo(args):
        @pl.when(halo_ok(args[0]))
        def _():
            halo(*args).start()

    def wait_halo(args):
        @pl.when(halo_ok(1 - args[0]))
        def _():
            halo(*args).wait_recv()

    def drain_halo(args):
        @pl.when(halo_ok(args[0]))
        def _():
            halo(*args).wait_send()

    def lanes_of(buf, rows):
        return jnp.concatenate([buf[i, rows, :] for i in range(H)], axis=1)

    for c in range(PARTS):
        chain_step(c, grid_view(c), H - 1)
        rows = pl.ds(c * chunk, chunk)
        normed = normalize(lanes_of(grid_buf, rows).astype(F32))
        made = dot(normed, a_buf[:, 0 : 3 * cols])
        kv[pl.ds(rim + c * chunk, chunk), :] = made[:, : 2 * cols].astype(BF16)
        gq[rows, :] = (made[:, 2 * cols :] * scaling).astype(BF16)
        start_halo(halo_enc(c))
    chain_step(MESH_ITEM, whole(mesh_buf), H - 1)
    everything = pl.ds(0, mesh_rows)
    mesh_full = lanes_of(mesh_buf, everything).astype(F32)
    mesh_q = (dot(normalize(mesh_full), a_buf[:, 3 * cols :]) * scaling).astype(BF16)
    if gathers:
        chain_step(OUT_ITEM, whole(c_own), H - 1)
        for s in range(H):
            gather_start(2 + s, c_view(s), c_own.at[s])
        gather_pass(1, b_view)
    for c in range(PARTS):
        wait_halo(halo_enc(c))

    def blocks_of(buf, start, width):
        rows = pl.ds(start * TILE, width * TILE)
        return buf[rows, 0:cols], buf[rows, cols : 2 * cols]

    def place_of(width):
        return lax.broadcasted_iota(jnp.int32, (1, width * TILE), 1) // TILE

    def live_slots(place, blocks, live_count):
        left = jnp.zeros(place.shape, jnp.int32)
        for s, block in enumerate(blocks):
            left = jnp.where(place == block, live_count - s, left)
        return left > 0

    base = n * grid_tiles - rim // TILE
    width = eb.shape[1]
    reach = (grid_rows + 2 * rim) // TILE
    place = place_of(reach)
    key, value = blocks_of(kv, 0, reach)
    for t in range(mesh_tiles):
        mask = live_slots(place, [eb[t, s] - base for s in range(width)], ec[t])
        enc_buf[h, pl.ds(t * TILE, TILE), :] = attend(
            mesh_q[t * TILE : (t + 1) * TILE], key, value, mask
        )
    chain_start(ENC_ITEM, whole(enc_buf))
    if gathers:
        for s in range(H):
            gather_pass(2 + s, c_view(s))
        gather_wait(1, b_view)
    for s in range(1, H):
        chain_step(ENC_ITEM, whole(enc_buf), s)
    if gathers:
        for s in range(H):
            gather_wait(2 + s, c_view(s))

    def out_weight(k, rows):
        return jnp.concatenate(
            [c_buf[i, rows, k * cols : (k + 1) * cols] for i in range(H)], axis=1
        )

    all_features = pl.ds(0, H * part_features)
    mesh_one = (
        mesh_full + dot_t(lanes_of(enc_buf, everything), out_weight(0, all_features))
    ).astype(BF16)
    made = dot(normalize(mesh_one.astype(F32)), b_buf[:, 0 : 3 * cols])
    window_q = (made[:, :cols] * scaling).astype(BF16)
    wkv[pl.ds(mesh_rows, mesh_rows), :] = made[:, cols:].astype(BF16)
    own = wkv.at[pl.ds(mesh_rows, mesh_rows), :]
    window_halo = [
        (0, rim_parts, own, wkv.at[pl.ds(2 * mesh_rows, mesh_rows), :]),
        (1, rim_parts, own, wkv.at[pl.ds(0, mesh_rows), :]),
    ]
    for args in window_halo:
        start_halo(args)
    for args in window_halo:
        wait_halo(args)
    width = wo.shape[1]
    for t in range(mesh_tiles):
        key, value = blocks_of(wkv, t, 2 * mesh_tiles + 1)
        place = place_of(2 * mesh_tiles + 1)
        reached = n * mesh_tiles + t - mesh_tiles + place
        chosen = live_slots(place, [mesh_tiles + wo[t, s] for s in range(width)], width)
        mask = chosen & (reached >= 0) & (reached < mesh_tiles * N)
        win_buf[h, pl.ds(t * TILE, TILE), :] = attend(
            window_q[t * TILE : (t + 1) * TILE], key, value, mask
        )
    chain_start(WIN_ITEM, whole(win_buf))
    for s in range(1, H):
        chain_step(WIN_ITEM, whole(win_buf), s)
    mesh_two = (
        mesh_one.astype(F32) + dot_t(lanes_of(win_buf, everything), out_weight(1, all_features))
    ).astype(BF16)
    for i in range(H):
        two_buf[i] = mesh_two[:, i * part_features : (i + 1) * part_features]
    units = (b_buf.shape[1] - 5 * cols) // 2
    first = 3 * cols
    hidden = dot(normalize(mesh_two.astype(F32)), b_buf[:, first : first + units])
    hidden = (0.5 * hidden * (1.0 + lax.erf(hidden * (0.5**0.5)))).astype(BF16)
    last = 5 * cols + units

    def term(lane):
        rows = pl.ds(pl.multiple_of(lane * part_features, part_features), part_features)
        return dot_t(hidden, b_buf[rows, last : last + units])

    def part_copy(d, lane):
        return copy(rs_src.at[d], rs_dst.at[d], rs_s.at[d], rs_r.at[d], (n, lane))

    for d in range(1, H):
        lane = lax.rem(h + d, H)
        rs_src[d] = term(lane).astype(BF16)
        part_copy(d, lane).start()
    total = two_buf[h].astype(F32) + term(h)
    for d in range(1, H):
        part_copy(d, lax.rem(h + d, H)).wait_recv()
        total = total + rs_dst[d].astype(F32)
    three = total.astype(BF16)
    three_buf[h] = three
    chain_start(THREE_ITEM, whole(three_buf))
    mesh_out[...] = three
    for s in range(1, H):
        chain_step(THREE_ITEM, whole(three_buf), s)
    mesh_norm = normalize(lanes_of(three_buf, everything).astype(F32))
    made = dot(mesh_norm, b_buf[:, first + units : last])
    dkv[pl.ds(TILE, mesh_rows), :] = made.astype(BF16)
    decoder_halo = [
        (0, rim_parts + 1, dkv.at[pl.ds(TILE, TILE), :], dkv.at[pl.ds(TILE + mesh_rows, TILE), :]),
        (1, rim_parts + 1, dkv.at[pl.ds(mesh_rows, TILE), :], dkv.at[pl.ds(0, TILE), :]),
    ]
    for args in decoder_halo:
        start_halo(args)
    for args in decoder_halo:
        wait_halo(args)
    base_mesh = n * mesh_tiles - 1
    width = db.shape[1]
    place = place_of(mesh_tiles + 2)
    key, value = blocks_of(dkv, 0, mesh_tiles + 2)
    per_part = grid_tiles // PARTS
    for c in range(PARTS):
        for u in range(per_part):
            g = c * per_part + u
            mask = live_slots(place, [db[g, s] - base_mesh for s in range(width)], dc[g])
            rows = pl.ds(g * TILE, TILE)
            dec_buf[h, rows, :] = attend(gq[rows, :], key, value, mask)
        chain_start(DEC_ITEM + c, dec_view(c))
    mine = pl.ds(pl.multiple_of(h * part_features, part_features), part_features)
    dec_weight = out_weight(2, mine)
    for s in range(1, H - 1):
        for c in range(PARTS):
            chain_step(DEC_ITEM + c, dec_view(c), s)
    for c in range(PARTS):
        chain_step(DEC_ITEM + c, dec_view(c), H - 1)
        rows = pl.ds(c * chunk, chunk)
        update = dot_t(lanes_of(dec_buf, rows), dec_weight)
        grid_out[rows, :] = (grid_in[rows, :].astype(F32) + update).astype(BF16)

    for c in range(PARTS):
        chain_drain(c, grid_view(c))
        chain_drain(DEC_ITEM + c, dec_view(c))
        drain_halo(halo_enc(c))
    chain_drain(MESH_ITEM, whole(mesh_buf))
    chain_drain(ENC_ITEM, whole(enc_buf))
    chain_drain(WIN_ITEM, whole(win_buf))
    chain_drain(THREE_ITEM, whole(three_buf))
    for args in window_halo + decoder_halo:
        drain_halo(args)
    for d in range(1, H):
        part_copy(d, lax.rem(h + d, H)).wait_send()
    if gathers:
        chain_drain(OUT_ITEM, whole(c_own))
        gather_drain(0, a_view)
        gather_drain(1, b_view)
        for s in range(H):
            gather_drain(2 + s, c_view(s))


def local(
    grid_state, mesh_state,
    encoder_query, encoder_key, encoder_value, encoder_output,
    window_query, window_key, window_value, window_output,
    expand_weight, shrink_weight,
    decoder_query, decoder_key, decoder_value, decoder_output,
    encoder_blocks, encoder_count, window_offsets, decoder_blocks, decoder_count,
):
    N, H = lax.axis_size("nodes"), lax.axis_size("heads")
    grid_rows, part = grid_state.shape
    mesh_rows = mesh_state.shape[0]
    shard, cols = encoder_key.shape
    features = part * H
    a = jnp.concatenate([encoder_key, encoder_value, decoder_query, encoder_query], axis=1)
    b = jnp.concatenate(
        [
            window_query, window_key, window_value, expand_weight,
            decoder_key, decoder_value, shrink_weight.T,
        ],
        axis=1,
    )
    c = jnp.concatenate([encoder_output.T, window_output.T, decoder_output.T], axis=1)
    gathers = N % 2 == 0 and shard % 16 == 0
    if not gathers:
        a = lax.all_gather(a, "nodes", axis=0, tiled=True)
        b = lax.all_gather(b, "nodes", axis=0, tiled=True)
        c = lax.all_gather(c, "nodes", axis=0, tiled=True)
        c = lax.all_gather(c, "heads", axis=0, tiled=False)
    V = pltpu.VMEM
    DMA = pltpu.SemaphoreType.DMA
    scratch = []
    if gathers:
        scratch += [
            V((features, a.shape[1]), BF16),
            V((features, b.shape[1]), BF16),
            V((H,) + c.shape, BF16),
            V((H, features, c.shape[1]), BF16),
        ]
    items = 2 * PARTS + 5
    scratch += [
        V((H, grid_rows, part), BF16),
        V((2 * grid_rows, 2 * cols), BF16),
        V((grid_rows, cols), BF16),
        V((H, mesh_rows, part), BF16),
        V((H, mesh_rows, cols), BF16),
        V((H, mesh_rows, cols), BF16),
        V((H, mesh_rows, part), BF16),
        V((3 * mesh_rows, 2 * cols), BF16),
        V((H, mesh_rows, part), BF16),
        V((H, mesh_rows, part), BF16),
        V((H, mesh_rows, part), BF16),
        V((mesh_rows + 2 * TILE, 2 * cols), BF16),
        V((H, grid_rows, cols), BF16),
        DMA((2, items, H)),
        DMA((items, H)),
        DMA((2, PARTS // 2 + 2)),
        DMA((2, PARTS // 2 + 2)),
        DMA((H,)),
        DMA((H,)),
    ]
    if gathers:
        scratch += [DMA((2 + H, N // 2)), DMA((2 + H, N)), DMA((2 + H, N))]
    smem = pl.BlockSpec(memory_space=pltpu.SMEM)
    vmem = pl.BlockSpec(memory_space=pltpu.VMEM)
    return pl.pallas_call(
        functools.partial(kernel, N, H, gathers),
        out_shape=(
            jax.ShapeDtypeStruct(grid_state.shape, BF16),
            jax.ShapeDtypeStruct(mesh_state.shape, BF16),
        ),
        in_specs=[smem] * 5 + [vmem] * 5,
        out_specs=(vmem, vmem),
        scratch_shapes=scratch,
        compiler_params=pltpu.CompilerParams(
            collective_id=0, has_side_effects=True, vmem_limit_bytes=56 * 2**20
        ),
    )(
        encoder_blocks, encoder_count, window_offsets, decoder_blocks, decoder_count,
        grid_state, mesh_state, a, b, c,
    )


def solution(mesh):
    rows, columns = P("nodes", "heads"), P("heads", "nodes")
    in_specs = (
        (rows,) * 5 + (columns,) + (rows,) * 3 + (columns,) + (rows, columns)
        + (rows,) * 3 + (columns,)
        + (P("nodes", None), P("nodes"), P("nodes", None), P("nodes", None), P("nodes"))
    )
    return jax.shard_map(
        local, mesh=mesh, in_specs=in_specs, out_specs=(rows, rows), check_vma=False
    )
```

```python
import functools

import jax
import jax.numpy as jnp
from jax import lax
from jax.experimental import pallas as pl
from jax.experimental.pallas import tpu as pltpu
from jax.sharding import PartitionSpec as P

HEAD_DIM = 64
TILE = 128
EPSILON = 1e-05
PARTS = 4
MESH = pl.DeviceIdType.MESH
F32 = jnp.float32
BF16 = jnp.bfloat16


def normalize(values):
    average = jnp.mean(values, axis=-1, keepdims=True)
    centred = values - average
    spread = jnp.mean(centred * centred, axis=-1, keepdims=True)
    return (centred * lax.rsqrt(spread + EPSILON)).astype(BF16)


def dot(a, b):
    return jnp.dot(a, b, preferred_element_type=F32)


def dot_t(a, b):
    return lax.dot_general(a, b, (((1,), (1,)), ((), ())), preferred_element_type=F32)


def attend(query, key, value, mask):
    columns = query.shape[1]
    heads = columns // HEAD_DIM
    lane = lax.broadcasted_iota(jnp.int32, (1, columns), 1) // HEAD_DIM
    query = query.astype(F32)
    stacked = jnp.concatenate(
        [jnp.where(lane == i, query, 0.0) for i in range(heads)], axis=0
    ).astype(BF16)
    scores = dot_t(stacked, key)
    scores = jnp.where(mask, scores, -1e30)
    weights = jnp.exp(scores - jnp.max(scores, axis=-1, keepdims=True))
    weights = (weights * (1.0 / jnp.sum(weights, axis=-1, keepdims=True))).astype(BF16)
    mixed = dot(weights, value)
    rows = query.shape[0]
    result = mixed[:rows]
    for i in range(1, heads):
        result = jnp.where(lane == i, mixed[i * rows : (i + 1) * rows], result)
    return result.astype(BF16)


def kernel(count, lanes, gathers, *refs):
    N, H = count, lanes
    eb, ec, wo, db, dc = refs[:5]
    refs = refs[5:]
    if gathers:
        (
            grid_in, mesh_in, eq_in, ek_in, ev_in, eo_in, wq_in, wk_in, wv_in, wout_in,
            ex_in, sh_in, dq_in, dk_in, dv_in, dout_in,
        ) = refs[:16]
        grid_out, mesh_out = refs[16:18]
        a_buf, b_buf, s_buf, o_own, o_buf, loads = refs[18:24]
        refs = refs[24:]
    else:
        grid_in, mesh_in, a_buf, b_buf, s_buf, o_buf = refs[:6]
        grid_out, mesh_out = refs[6:8]
        loads = refs[8]
        refs = refs[9:]
    (
        grid_buf, kv, gq, mesh_buf, enc_buf, win_buf, two_buf, wkv, rs_src, rs_dst,
        three_buf, dkv, dec_buf, zs, zr, hs, hr, rs_s, rs_r,
    ) = refs[:19]
    if gathers:
        ns, nf, nr = refs[19:]
    scaling = HEAD_DIM ** (-0.5)
    n = lax.axis_index("nodes")
    h = lax.axis_index("heads")
    grid_rows, part_features = grid_in.shape
    mesh_rows = mesh_in.shape[0]
    chunk = grid_rows // PARTS
    rim = grid_rows // 2
    grid_tiles, mesh_tiles = grid_rows // TILE, mesh_rows // TILE
    cols = gq.shape[1]

    copies = []

    def load(src, dst):
        copies.append(pltpu.make_async_copy(src, dst, loads.at[len(copies)]))
        copies[-1].start()

    def placed(buf, size, column, src):
        rows = pl.ds(pl.multiple_of(n * size, size), size)
        load(src, buf.at[rows, pl.ds(column, src.shape[1])])

    load(grid_in, grid_buf.at[h])
    load(mesh_in, mesh_buf.at[h])
    if gathers:
        shard = ek_in.shape[0]
        for k, src in enumerate((ek_in, ev_in, dq_in, eq_in)):
            placed(a_buf, shard, k * cols, src)
        for k, src in enumerate((eo_in, wout_in, dout_in)):
            load(src, o_own.at[k, h])
        column = 0
        for src in (wq_in, wk_in, wv_in, ex_in, dk_in, dv_in):
            placed(b_buf, shard, column, src)
            column += src.shape[1]
        load(sh_in, s_buf.at[:, pl.ds(pl.multiple_of(n * shard, shard), shard)])

    barrier = pltpu.get_barrier_semaphore()

    def greet(node, lane):
        pl.semaphore_signal(barrier, inc=1, device_id=(node, lane), device_id_type=MESH)

    node_steps = range(1, N) if gathers else (1, N - 1)
    for d in node_steps:
        greet(lax.rem(n + d, N), h)
    for d in range(1, H):
        greet(n, lax.rem(h + d, H))
    pl.semaphore_wait(barrier, len(node_steps) + H - 1)

    def copy(src, dst, send, recv, device):
        return pltpu.make_async_remote_copy(
            src_ref=src, dst_ref=dst, send_sem=send, recv_sem=recv,
            device_id=device, device_id_type=MESH,
        )

    def link(item, src, dst, slot, way):
        lane = h + 1 if way == 0 else h - 1
        return copy(src, dst, zs.at[way, item, slot], zr.at[item, slot], (n, lane))

    def chain_start(item, view, src=None):
        src = view(h) if src is None else src

        @pl.when(h + 1 < H)
        def _():
            link(item, src, view(h), h, 0).start()

        @pl.when(h > 0)
        def _():
            link(item, src, view(h), h, 1).start()

    def chain_step(item, view, s):
        @pl.when(h >= s)
        def _():
            a = h - s
            link(item, view(a), view(a), a, 1).wait_recv()

            @pl.when(h + 1 < H)
            def _():
                link(item, view(a), view(a), a, 0).start()

        @pl.when(h + s < H)
        def _():
            b = h + s
            link(item, view(b), view(b), b, 0).wait_recv()

            @pl.when(h > 0)
            def _():
                link(item, view(b), view(b), b, 1).start()

    def chain_drain(item, view):
        for s in range(H):

            @pl.when((h >= s) & (h + 1 < H))
            def _():
                link(item, view(h - s), view(h - s), h - s, 0).wait_send()

            @pl.when((h + s < H) & (h > 0))
            def _():
                link(item, view(h + s), view(h + s), h + s, 1).wait_send()

    beside = n + 1 - 2 * lax.rem(n, 2)

    def gather_start(item, view, src=None):
        if src is None:
            src = view(n)
        else:
            view(n)[...] = src[...]
        for j in range(1, N // 2):
            peer = lax.rem(n + 2 * j, N)
            copy(src, view(n), ns.at[item, j], nr.at[item, n], (peer, h)).start()
        copy(src, view(n), nf.at[item, n], nr.at[item, n], (beside, h)).start()

    def gather_pass(item, view):
        for j in range(1, N // 2):
            m = lax.rem(n + N - 2 * j, N)
            forward = copy(view(m), view(m), nf.at[item, m], nr.at[item, m], (beside, h))
            forward.wait_recv()
            forward.start()

    def gather_wait(item, view):
        for j in range(N // 2):
            m = lax.rem(beside + N - 2 * j, N)
            copy(view(m), view(m), nf.at[item, m], nr.at[item, m], (beside, h)).wait_recv()

    def gather_drain(item, view):
        for j in range(N // 2):
            if j:
                copy(view(n), view(n), ns.at[item, j], nr.at[item, n], (beside, h)).wait_send()
            m = lax.rem(n + N - 2 * j, N)
            copy(view(m), view(m), nf.at[item, m], nr.at[item, m], (beside, h)).wait_send()

    def rows_of(buf, size):
        return lambda m: buf.at[pl.ds(pl.multiple_of(m * size, size), size), :]

    def grid_view(c):
        return lambda s: grid_buf.at[s, pl.ds(c * chunk, chunk), :]

    def dec_view(c):
        return lambda s: dec_buf.at[s, pl.ds(c * chunk, chunk), :]

    whole = lambda buf: (lambda s: buf.at[s])
    MESH_ITEM, ENC_ITEM, WIN_ITEM, THREE_ITEM = range(PARTS, PARTS + 4)
    DEC_ITEM = PARTS + 4
    OUT_ITEM = 2 * PARTS + 4

    def halo(way, k, src, dst):
        node = n - 1 if way == 0 else n + 1
        return copy(src, dst, hs.at[way, k], hr.at[way, k], (node, h))

    def halo_ok(way):
        return n > 0 if way == 0 else n + 1 < N

    for one in copies:
        one.wait()
    if gathers:
        a_view, b_view = rows_of(a_buf, shard), rows_of(b_buf, shard)
        s_view = lambda m: s_buf.at[:, pl.ds(pl.multiple_of(m * shard, shard), shard)]
        o_chain = lambda k: (lambda s: o_own.at[k, s])

        def o_view(k, s):
            return lambda m: o_buf.at[
                k, pl.ds(s * cols, cols), pl.ds(pl.multiple_of(m * shard, shard), shard)
            ]

        gather_start(0, a_view)
        chain_start(OUT_ITEM, o_chain(0))
    for c in range(PARTS):
        chain_start(c, grid_view(c))
    chain_start(MESH_ITEM, whole(mesh_buf))
    if gathers:
        gather_start(1, b_view)
        gather_start(2, s_view)

    def out_items(k):
        return [(3 + k * H + s, o_view(k, s), o_own.at[k, s]) for s in range(H)]

    @pl.when(n == 0)
    def _():
        kv[0:rim, :] = jnp.zeros((rim, 2 * cols), BF16)
        wkv[0:mesh_rows, :] = jnp.zeros((mesh_rows, 2 * cols), BF16)
        dkv[0:TILE, :] = jnp.zeros((TILE, 2 * cols), BF16)

    @pl.when(n == N - 1)
    def _():
        kv[rim + grid_rows :, :] = jnp.zeros((rim, 2 * cols), BF16)
        wkv[2 * mesh_rows :, :] = jnp.zeros((mesh_rows, 2 * cols), BF16)
        dkv[TILE + mesh_rows :, :] = jnp.zeros((TILE, 2 * cols), BF16)

    for s in range(1, H - 1):
        if gathers:
            chain_step(OUT_ITEM, o_chain(0), s)
        for c in range(PARTS):
            if s == 1 and c == 1 and gathers:
                gather_pass(0, a_view)
            chain_step(c, grid_view(c), s)
        chain_step(MESH_ITEM, whole(mesh_buf), s)
    if gathers:
        chain_step(OUT_ITEM, o_chain(0), H - 1)
        for item in out_items(0):
            gather_start(*item)
        for k in (1, 2):
            chain_start(OUT_ITEM + k, o_chain(k))
        gather_wait(0, a_view)

    rim_parts = PARTS // 2

    def halo_enc(c):
        here = kv.at[pl.ds(rim + c * chunk, chunk), :]
        if c < rim_parts:
            return 0, c, here, kv.at[pl.ds(rim + grid_rows + c * chunk, chunk), :]
        k = c - rim_parts
        return 1, k, here, kv.at[pl.ds(k * chunk, chunk), :]

    def start_halo(args):
        @pl.when(halo_ok(args[0]))
        def _():
            halo(*args).start()

    def wait_halo(args):
        @pl.when(halo_ok(1 - args[0]))
        def _():
            halo(*args).wait_recv()

    def drain_halo(args):
        @pl.when(halo_ok(args[0]))
        def _():
            halo(*args).wait_send()

    def lanes_of(buf, rows):
        return jnp.concatenate([buf[i, rows, :] for i in range(H)], axis=1)

    for c in range(PARTS):
        chain_step(c, grid_view(c), H - 1)
        rows = pl.ds(c * chunk, chunk)
        normed = normalize(lanes_of(grid_buf, rows).astype(F32))
        made = dot(normed, a_buf[:, 0 : 3 * cols])
        kv[pl.ds(rim + c * chunk, chunk), :] = made[:, : 2 * cols].astype(BF16)
        gq[rows, :] = (made[:, 2 * cols :] * scaling).astype(BF16)
        start_halo(halo_enc(c))
    chain_step(MESH_ITEM, whole(mesh_buf), H - 1)
    everything = pl.ds(0, mesh_rows)
    mesh_full = lanes_of(mesh_buf, everything).astype(F32)
    mesh_q = (dot(normalize(mesh_full), a_buf[:, 3 * cols :]) * scaling).astype(BF16)
    def pass_out(s):
        if gathers:
            for k in (1, 2):
                chain_step(OUT_ITEM + k, o_chain(k), s)

    for s in range(1, H - 2):
        pass_out(s)
    if gathers:
        gather_pass(1, b_view)
        gather_pass(2, s_view)
        for item in out_items(0):
            gather_pass(*item[:2])
    for c in range(PARTS):
        wait_halo(halo_enc(c))
    pass_out(H - 2)

    def blocks_of(buf, start, width):
        rows = pl.ds(start * TILE, width * TILE)
        return buf[rows, 0:cols], buf[rows, cols : 2 * cols]

    def place_of(width):
        return lax.broadcasted_iota(jnp.int32, (1, width * TILE), 1) // TILE

    def live_slots(place, blocks, live_count):
        left = jnp.zeros(place.shape, jnp.int32)
        for s, block in enumerate(blocks):
            left = jnp.where(place == block, live_count - s, left)
        return left > 0

    base = n * grid_tiles - rim // TILE
    width = eb.shape[1]
    reach = (grid_rows + 2 * rim) // TILE
    place = place_of(reach)
    key, value = blocks_of(kv, 0, reach)
    for t in range(mesh_tiles):
        mask = live_slots(place, [eb[t, s] - base for s in range(width)], ec[t])
        enc_buf[h, pl.ds(t * TILE, TILE), :] = attend(
            mesh_q[t * TILE : (t + 1) * TILE], key, value, mask
        )
    chain_start(ENC_ITEM, whole(enc_buf))
    pass_out(H - 1)
    if gathers:
        for k in (1, 2):
            for item in out_items(k):
                gather_start(*item)
        gather_wait(1, b_view)
    for s in range(1, H):
        chain_step(ENC_ITEM, whole(enc_buf), s)
    if gathers:
        for item in out_items(0):
            gather_wait(*item[:2])

    mesh_one = (
        mesh_full + dot(lanes_of(enc_buf, everything), o_buf[0])
    ).astype(BF16)
    made = dot(normalize(mesh_one.astype(F32)), b_buf[:, 0 : 3 * cols])
    window_q = (made[:, :cols] * scaling).astype(BF16)
    wkv[pl.ds(mesh_rows, mesh_rows), :] = made[:, cols:].astype(BF16)
    own = wkv.at[pl.ds(mesh_rows, mesh_rows), :]
    window_halo = [
        (0, rim_parts, own, wkv.at[pl.ds(2 * mesh_rows, mesh_rows), :]),
        (1, rim_parts, own, wkv.at[pl.ds(0, mesh_rows), :]),
    ]
    for args in window_halo:
        start_halo(args)
    if gathers:
        for item in out_items(1):
            gather_pass(*item[:2])
    for args in window_halo:
        wait_halo(args)
    width = wo.shape[1]
    for t in range(mesh_tiles):
        key, value = blocks_of(wkv, t, 2 * mesh_tiles + 1)
        place = place_of(2 * mesh_tiles + 1)
        reached = n * mesh_tiles + t - mesh_tiles + place
        chosen = live_slots(place, [mesh_tiles + wo[t, s] for s in range(width)], width)
        mask = chosen & (reached >= 0) & (reached < mesh_tiles * N)
        win_buf[h, pl.ds(t * TILE, TILE), :] = attend(
            window_q[t * TILE : (t + 1) * TILE], key, value, mask
        )
    chain_start(WIN_ITEM, whole(win_buf))
    for s in range(1, H):
        chain_step(WIN_ITEM, whole(win_buf), s)
    if gathers:
        for item in out_items(1):
            gather_wait(*item[:2])
    mesh_two = (
        mesh_one.astype(F32) + dot(lanes_of(win_buf, everything), o_buf[1])
    ).astype(BF16)
    for i in range(H):
        two_buf[i] = mesh_two[:, i * part_features : (i + 1) * part_features]
    units = b_buf.shape[1] - 5 * cols
    first = 3 * cols
    hidden = dot(normalize(mesh_two.astype(F32)), b_buf[:, first : first + units])
    hidden = (0.5 * hidden * (1.0 + lax.erf(hidden * (0.5**0.5)))).astype(BF16)
    if gathers:
        gather_wait(2, s_view)

    def term(lane):
        mine = pl.ds(pl.multiple_of(lane * part_features, part_features), part_features)
        return dot(hidden, s_buf[:, mine])

    def part_copy(d, lane):
        return copy(rs_src.at[d], rs_dst.at[d], rs_s.at[d], rs_r.at[d], (n, lane))

    for d in range(1, H):
        lane = lax.rem(h + d, H)
        rs_src[d] = term(lane).astype(BF16)
        part_copy(d, lane).start()
    total = two_buf[h].astype(F32) + term(h)
    for d in range(1, H):
        part_copy(d, lax.rem(h + d, H)).wait_recv()
        total = total + rs_dst[d].astype(F32)
    three = total.astype(BF16)
    three_buf[h] = three
    chain_start(THREE_ITEM, whole(three_buf))
    mesh_out[...] = three
    if gathers:
        for item in out_items(2):
            gather_pass(*item[:2])
    for s in range(1, H):
        chain_step(THREE_ITEM, whole(three_buf), s)
    mesh_norm = normalize(lanes_of(three_buf, everything).astype(F32))
    made = dot(mesh_norm, b_buf[:, first + units :])
    dkv[pl.ds(TILE, mesh_rows), :] = made.astype(BF16)
    decoder_halo = [
        (0, rim_parts + 1, dkv.at[pl.ds(TILE, TILE), :], dkv.at[pl.ds(TILE + mesh_rows, TILE), :]),
        (1, rim_parts + 1, dkv.at[pl.ds(mesh_rows, TILE), :], dkv.at[pl.ds(0, TILE), :]),
    ]
    for args in decoder_halo:
        start_halo(args)
    for args in decoder_halo:
        wait_halo(args)
    base_mesh = n * mesh_tiles - 1
    width = db.shape[0]
    place = place_of(mesh_tiles + 2)
    key, value = blocks_of(dkv, 0, mesh_tiles + 2)
    per_part = grid_tiles // PARTS
    for c in range(PARTS):
        for u in range(per_part):
            g = c * per_part + u
            mask = live_slots(place, [db[s, g] - base_mesh for s in range(width)], dc[g])
            rows = pl.ds(g * TILE, TILE)
            dec_buf[h, rows, :] = attend(gq[rows, :], key, value, mask)
        chain_start(DEC_ITEM + c, dec_view(c))
    mine = pl.ds(pl.multiple_of(h * part_features, part_features), part_features)
    if gathers:
        for item in out_items(2):
            gather_wait(*item[:2])
    dec_weight = o_buf[2, :, mine]
    for s in range(1, H - 1):
        for c in range(PARTS):
            chain_step(DEC_ITEM + c, dec_view(c), s)
    for c in range(PARTS):
        chain_step(DEC_ITEM + c, dec_view(c), H - 1)
        rows = pl.ds(c * chunk, chunk)
        update = dot(lanes_of(dec_buf, rows), dec_weight)
        grid_out[rows, :] = (grid_buf[h, rows, :].astype(F32) + update).astype(BF16)

    for c in range(PARTS):
        chain_drain(c, grid_view(c))
        chain_drain(DEC_ITEM + c, dec_view(c))
        drain_halo(halo_enc(c))
    chain_drain(MESH_ITEM, whole(mesh_buf))
    chain_drain(ENC_ITEM, whole(enc_buf))
    chain_drain(WIN_ITEM, whole(win_buf))
    chain_drain(THREE_ITEM, whole(three_buf))
    for args in window_halo + decoder_halo:
        drain_halo(args)
    for d in range(1, H):
        part_copy(d, lax.rem(h + d, H)).wait_send()
    if gathers:
        for k in range(3):
            chain_drain(OUT_ITEM + k, o_chain(k))
            for item in out_items(k):
                gather_drain(*item[:2])
        gather_drain(0, a_view)
        gather_drain(1, b_view)
        gather_drain(2, s_view)


def local(
    grid_state, mesh_state,
    encoder_query, encoder_key, encoder_value, encoder_output,
    window_query, window_key, window_value, window_output,
    expand_weight, shrink_weight,
    decoder_query, decoder_key, decoder_value, decoder_output,
    encoder_blocks, encoder_count, window_offsets, decoder_blocks, decoder_count,
):
    N, H = lax.axis_size("nodes"), lax.axis_size("heads")
    grid_rows, part = grid_state.shape
    mesh_rows = mesh_state.shape[0]
    shard, cols = encoder_key.shape
    features = part * H
    gathers = N % 2 == 0 and shard % 128 == 0
    V = pltpu.VMEM
    DMA = pltpu.SemaphoreType.DMA
    units = expand_weight.shape[1]
    if gathers:
        weights = (
            encoder_query, encoder_key, encoder_value, encoder_output,
            window_query, window_key, window_value, window_output,
            expand_weight, shrink_weight,
            decoder_query, decoder_key, decoder_value, decoder_output,
        )
        scratch = [
            V((features, 4 * cols), BF16),
            V((features, 5 * cols + units), BF16),
            V((units, features), BF16),
            V((3, H, cols, shard), BF16),
            V((3, H * cols, features), BF16),
        ]
    else:
        a = jnp.concatenate([encoder_key, encoder_value, decoder_query, encoder_query], axis=1)
        b = jnp.concatenate(
            [
                window_query, window_key, window_value, expand_weight,
                decoder_key, decoder_value,
            ],
            axis=1,
        )
        out = jnp.stack([encoder_output, window_output, decoder_output])
        weights = (
            lax.all_gather(a, "nodes", axis=0, tiled=True),
            lax.all_gather(b, "nodes", axis=0, tiled=True),
            lax.all_gather(shrink_weight, "nodes", axis=1, tiled=True),
            lax.all_gather(
                lax.all_gather(out, "nodes", axis=2, tiled=True), "heads", axis=1, tiled=True
            ),
        )
        scratch = []
    scratch += [DMA((16,))]
    items = 2 * PARTS + 7
    scratch += [
        V((H, grid_rows, part), BF16),
        V((2 * grid_rows, 2 * cols), BF16),
        V((grid_rows, cols), BF16),
        V((H, mesh_rows, part), BF16),
        V((H, mesh_rows, cols), BF16),
        V((H, mesh_rows, cols), BF16),
        V((H, mesh_rows, part), BF16),
        V((3 * mesh_rows, 2 * cols), BF16),
        V((H, mesh_rows, part), BF16),
        V((H, mesh_rows, part), BF16),
        V((H, mesh_rows, part), BF16),
        V((mesh_rows + 2 * TILE, 2 * cols), BF16),
        V((H, grid_rows, cols), BF16),
        DMA((2, items, H)),
        DMA((items, H)),
        DMA((2, PARTS // 2 + 2)),
        DMA((2, PARTS // 2 + 2)),
        DMA((H,)),
        DMA((H,)),
    ]
    if gathers:
        scratch += [DMA((3 + 3 * H, N // 2)), DMA((3 + 3 * H, N)), DMA((3 + 3 * H, N))]
    smem = pl.BlockSpec(memory_space=pltpu.SMEM)
    vmem = pl.BlockSpec(memory_space=pltpu.VMEM)
    hbm = pl.BlockSpec(memory_space=pl.ANY)
    kept = [hbm] * len(weights) if gathers else [vmem] * len(weights)
    return pl.pallas_call(
        functools.partial(kernel, N, H, gathers),
        out_shape=(
            jax.ShapeDtypeStruct(grid_state.shape, BF16),
            jax.ShapeDtypeStruct(mesh_state.shape, BF16),
        ),
        in_specs=[smem] * 5 + [hbm] * 2 + kept,
        out_specs=(vmem, vmem),
        scratch_shapes=scratch,
        compiler_params=pltpu.CompilerParams(
            collective_id=0, has_side_effects=True
        ),
    )(
        encoder_blocks, encoder_count, window_offsets, decoder_blocks.T, decoder_count,
        grid_state, mesh_state, *weights,
    )


def solution(mesh):
    rows, columns = P("nodes", "heads"), P("heads", "nodes")
    in_specs = (
        (rows,) * 5 + (columns,) + (rows,) * 3 + (columns,) + (rows, columns)
        + (rows,) * 3 + (columns,)
        + (P("nodes", None), P("nodes"), P("nodes", None), P("nodes", None), P("nodes"))
    )
    return jax.shard_map(
        local, mesh=mesh, in_specs=in_specs, out_specs=(rows, rows), check_vma=False
    )
```

```python
import functools

import jax
import jax.numpy as jnp
from jax import lax
from jax.experimental import pallas as pl
from jax.experimental.pallas import tpu as pltpu
from jax.sharding import PartitionSpec as P

HEAD_DIM = 64
TILE = 128
EPSILON = 1e-05
PARTS = 4
MESH = pl.DeviceIdType.MESH
F32 = jnp.float32
BF16 = jnp.bfloat16


def normalize(values):
    average = jnp.mean(values, axis=-1, keepdims=True)
    centred = values - average
    spread = jnp.mean(centred * centred, axis=-1, keepdims=True)
    return (centred * lax.rsqrt(spread + EPSILON)).astype(BF16)


def dot(a, b):
    return jnp.dot(a, b, preferred_element_type=F32)


def dot_t(a, b):
    return lax.dot_general(a, b, (((1,), (1,)), ((), ())), preferred_element_type=F32)


def attend(query, key, value, mask):
    columns = query.shape[1]
    heads = columns // HEAD_DIM
    lane = lax.broadcasted_iota(jnp.int32, (1, columns), 1) // HEAD_DIM
    query = query.astype(F32)
    stacked = jnp.concatenate(
        [jnp.where(lane == i, query, 0.0) for i in range(heads)], axis=0
    ).astype(BF16)
    scores = dot_t(stacked, key)
    scores = jnp.where(mask, scores, -1e30)
    weights = jnp.exp(scores - jnp.max(scores, axis=-1, keepdims=True))
    weights = (weights * (1.0 / jnp.sum(weights, axis=-1, keepdims=True))).astype(BF16)
    mixed = dot(weights, value)
    rows = query.shape[0]
    result = mixed[:rows]
    for i in range(1, heads):
        result = jnp.where(lane == i, mixed[i * rows : (i + 1) * rows], result)
    return result.astype(BF16)


def kernel(count, lanes, gathers, *refs):
    N, H = count, lanes
    eb, ec, wo, db, dc = refs[:5]
    refs = refs[5:]
    if gathers:
        (
            grid_in, mesh_in, eq_in, ek_in, ev_in, eo_in, wq_in, wk_in, wv_in, wout_in,
            ex_in, sh_in, dq_in, dk_in, dv_in, dout_in,
        ) = refs[:16]
        grid_out, mesh_out = refs[16:18]
        a_buf, b_buf, s_buf, o_own, o_buf, loads = refs[18:24]
        refs = refs[24:]
    else:
        grid_in, mesh_in, a_buf, b_buf, s_buf, o_buf = refs[:6]
        grid_out, mesh_out = refs[6:8]
        loads = refs[8]
        refs = refs[9:]
    (
        grid_buf, kv, gq, mesh_buf, enc_buf, win_buf, two_buf, wkv, rs_src, rs_dst,
        three_buf, dkv, dec_buf, zs, zr, hs, hr, rs_s, rs_r,
    ) = refs[:19]
    if gathers:
        ns, nf, nr = refs[19:]
    scaling = HEAD_DIM ** (-0.5)
    n = lax.axis_index("nodes")
    h = lax.axis_index("heads")
    grid_rows, part_features = grid_in.shape
    mesh_rows = mesh_in.shape[0]
    chunk = grid_rows // PARTS
    rim = grid_rows // 2
    grid_tiles, mesh_tiles = grid_rows // TILE, mesh_rows // TILE
    cols = gq.shape[1]

    copies = []

    def load(src, dst):
        copies.append(pltpu.make_async_copy(src, dst, loads.at[len(copies)]))
        copies[-1].start()

    def placed(buf, size, column, src):
        rows = pl.ds(pl.multiple_of(n * size, size), size)
        load(src, buf.at[rows, pl.ds(column, src.shape[1])])

    load(grid_in, grid_buf.at[h])
    load(mesh_in, mesh_buf.at[h])
    if gathers:
        shard = ek_in.shape[0]
        for k, src in enumerate((ek_in, ev_in, dq_in, eq_in)):
            placed(a_buf, shard, k * cols, src)
        for k, src in enumerate((eo_in, wout_in, dout_in)):
            load(src, o_own.at[k, h])
        column = 0
        for src in (wq_in, wk_in, wv_in, ex_in, dk_in, dv_in):
            placed(b_buf, shard, column, src)
            column += src.shape[1]
        load(sh_in, s_buf.at[:, pl.ds(pl.multiple_of(n * shard, shard), shard)])

    barrier = pltpu.get_barrier_semaphore()

    def greet(node, lane):
        pl.semaphore_signal(barrier, inc=1, device_id=(node, lane), device_id_type=MESH)

    node_steps = range(1, N) if gathers else (1, N - 1)
    for d in node_steps:
        greet(lax.rem(n + d, N), h)
    for d in range(1, H):
        greet(n, lax.rem(h + d, H))
    pl.semaphore_wait(barrier, len(node_steps) + H - 1)

    def copy(src, dst, send, recv, device):
        return pltpu.make_async_remote_copy(
            src_ref=src, dst_ref=dst, send_sem=send, recv_sem=recv,
            device_id=device, device_id_type=MESH,
        )

    def link(item, src, dst, slot, way):
        lane = h + 1 if way == 0 else h - 1
        return copy(src, dst, zs.at[way, item, slot], zr.at[item, slot], (n, lane))

    def chain_start(item, view, src=None):
        src = view(h) if src is None else src

        @pl.when(h + 1 < H)
        def _():
            link(item, src, view(h), h, 0).start()

        @pl.when(h > 0)
        def _():
            link(item, src, view(h), h, 1).start()

    def chain_step(item, view, s):
        @pl.when(h >= s)
        def _():
            a = h - s
            link(item, view(a), view(a), a, 1).wait_recv()

            @pl.when(h + 1 < H)
            def _():
                link(item, view(a), view(a), a, 0).start()

        @pl.when(h + s < H)
        def _():
            b = h + s
            link(item, view(b), view(b), b, 0).wait_recv()

            @pl.when(h > 0)
            def _():
                link(item, view(b), view(b), b, 1).start()

    def chain_drain(item, view):
        for s in range(H):

            @pl.when((h >= s) & (h + 1 < H))
            def _():
                link(item, view(h - s), view(h - s), h - s, 0).wait_send()

            @pl.when((h + s < H) & (h > 0))
            def _():
                link(item, view(h + s), view(h + s), h + s, 1).wait_send()

    beside = n + 1 - 2 * lax.rem(n, 2)

    def gather_start(item, view, src=None):
        if src is None:
            src = view(n)
        else:
            view(n)[...] = src[...]
        for j in range(1, N // 2):
            peer = lax.rem(n + 2 * j, N)
            copy(src, view(n), ns.at[item, j], nr.at[item, n], (peer, h)).start()
        copy(src, view(n), nf.at[item, n], nr.at[item, n], (beside, h)).start()

    def gather_pass(item, view):
        for j in range(1, N // 2):
            m = lax.rem(n + N - 2 * j, N)
            forward = copy(view(m), view(m), nf.at[item, m], nr.at[item, m], (beside, h))
            forward.wait_recv()
            forward.start()

    def gather_wait(item, view):
        for j in range(N // 2):
            m = lax.rem(beside + N - 2 * j, N)
            copy(view(m), view(m), nf.at[item, m], nr.at[item, m], (beside, h)).wait_recv()

    def gather_drain(item, view):
        for j in range(N // 2):
            if j:
                copy(view(n), view(n), ns.at[item, j], nr.at[item, n], (beside, h)).wait_send()
            m = lax.rem(n + N - 2 * j, N)
            copy(view(m), view(m), nf.at[item, m], nr.at[item, m], (beside, h)).wait_send()

    def rows_of(buf, size):
        return lambda m: buf.at[pl.ds(pl.multiple_of(m * size, size), size), :]

    def grid_view(c):
        return lambda s: grid_buf.at[s, pl.ds(c * chunk, chunk), :]

    def dec_view(c):
        return lambda s: dec_buf.at[s, pl.ds(c * chunk, chunk), :]

    whole = lambda buf: (lambda s: buf.at[s])
    MESH_ITEM, ENC_ITEM, WIN_ITEM, THREE_ITEM = range(PARTS, PARTS + 4)
    DEC_ITEM = PARTS + 4
    OUT_ITEM = 2 * PARTS + 4
    TILE_ITEM = 2 * PARTS + 7

    def tile_items(buf, first):
        view = lambda t: (lambda s: buf.at[s, pl.ds(t * TILE, TILE), :])
        return [(TILE_ITEM + first + t, view(t)) for t in range(mesh_tiles)]

    enc_items, win_items = tile_items(enc_buf, 0), tile_items(win_buf, mesh_tiles)

    def halo(way, k, src, dst):
        node = n - 1 if way == 0 else n + 1
        return copy(src, dst, hs.at[way, k], hr.at[way, k], (node, h))

    def halo_ok(way):
        return n > 0 if way == 0 else n + 1 < N

    for one in copies:
        one.wait()
    if gathers:
        a_view, b_view = rows_of(a_buf, shard), rows_of(b_buf, shard)
        s_view = lambda m: s_buf.at[:, pl.ds(pl.multiple_of(m * shard, shard), shard)]
        o_chain = lambda k: (lambda s: o_own.at[k, s])

        def o_view(k, s):
            return lambda m: o_buf.at[
                k, pl.ds(s * cols, cols), pl.ds(pl.multiple_of(m * shard, shard), shard)
            ]

        gather_start(0, a_view)
        chain_start(OUT_ITEM, o_chain(0))
    for c in range(PARTS):
        chain_start(c, grid_view(c))
    chain_start(MESH_ITEM, whole(mesh_buf))
    if gathers:
        gather_start(1, b_view)
        gather_start(2, s_view)

    def out_items(k):
        return [(3 + k * H + s, o_view(k, s), o_own.at[k, s]) for s in range(H)]

    @pl.when(n == 0)
    def _():
        kv[0:rim, :] = jnp.zeros((rim, 2 * cols), BF16)
        wkv[0:mesh_rows, :] = jnp.zeros((mesh_rows, 2 * cols), BF16)
        dkv[0:TILE, :] = jnp.zeros((TILE, 2 * cols), BF16)

    @pl.when(n == N - 1)
    def _():
        kv[rim + grid_rows :, :] = jnp.zeros((rim, 2 * cols), BF16)
        wkv[2 * mesh_rows :, :] = jnp.zeros((mesh_rows, 2 * cols), BF16)
        dkv[TILE + mesh_rows :, :] = jnp.zeros((TILE, 2 * cols), BF16)

    for s in range(1, H - 1):
        if gathers:
            chain_step(OUT_ITEM, o_chain(0), s)
        for c in range(PARTS):
            if s == 1 and c == 1 and gathers:
                gather_pass(0, a_view)
            chain_step(c, grid_view(c), s)
        chain_step(MESH_ITEM, whole(mesh_buf), s)
    if gathers:
        chain_step(OUT_ITEM, o_chain(0), H - 1)
        for item in out_items(0):
            gather_start(*item)
        for k in (1, 2):
            chain_start(OUT_ITEM + k, o_chain(k))
        gather_wait(0, a_view)

    rim_parts = PARTS // 2

    def halo_enc(c):
        here = kv.at[pl.ds(rim + c * chunk, chunk), :]
        if c < rim_parts:
            return 0, c, here, kv.at[pl.ds(rim + grid_rows + c * chunk, chunk), :]
        k = c - rim_parts
        return 1, k, here, kv.at[pl.ds(k * chunk, chunk), :]

    def start_halo(args):
        @pl.when(halo_ok(args[0]))
        def _():
            halo(*args).start()

    def wait_halo(args):
        @pl.when(halo_ok(1 - args[0]))
        def _():
            halo(*args).wait_recv()

    def drain_halo(args):
        @pl.when(halo_ok(args[0]))
        def _():
            halo(*args).wait_send()

    def lanes_of(buf, rows):
        return jnp.concatenate([buf[i, rows, :] for i in range(H)], axis=1)

    for c in range(PARTS):
        chain_step(c, grid_view(c), H - 1)
        rows = pl.ds(c * chunk, chunk)
        normed = normalize(lanes_of(grid_buf, rows).astype(F32))
        made = dot(normed, a_buf[:, 0 : 3 * cols])
        kv[pl.ds(rim + c * chunk, chunk), :] = made[:, : 2 * cols].astype(BF16)
        gq[rows, :] = (made[:, 2 * cols :] * scaling).astype(BF16)
        start_halo(halo_enc(c))
    chain_step(MESH_ITEM, whole(mesh_buf), H - 1)
    everything = pl.ds(0, mesh_rows)
    mesh_full = lanes_of(mesh_buf, everything).astype(F32)
    mesh_q = (dot(normalize(mesh_full), a_buf[:, 3 * cols :]) * scaling).astype(BF16)
    def pass_out(s):
        if gathers:
            for k in (1, 2):
                chain_step(OUT_ITEM + k, o_chain(k), s)

    for s in range(1, H - 2):
        pass_out(s)
    if gathers:
        gather_pass(1, b_view)
        gather_pass(2, s_view)
        for item in out_items(0):
            gather_pass(*item[:2])
    for c in range(PARTS):
        wait_halo(halo_enc(c))
    pass_out(H - 2)

    def blocks_of(buf, start, width):
        rows = pl.ds(start * TILE, width * TILE)
        return buf[rows, 0:cols], buf[rows, cols : 2 * cols]

    def place_of(width):
        return lax.broadcasted_iota(jnp.int32, (1, width * TILE), 1) // TILE

    def live_slots(place, blocks, live_count):
        left = jnp.zeros(place.shape, jnp.int32)
        for s, block in enumerate(blocks):
            left = jnp.where(place == block, live_count - s, left)
        return left > 0

    base = n * grid_tiles - rim // TILE
    width = eb.shape[1]
    reach = (grid_rows + 2 * rim) // TILE
    place = place_of(reach)
    key, value = blocks_of(kv, 0, reach)
    for t in range(mesh_tiles):
        mask = live_slots(place, [eb[t, s] - base for s in range(width)], ec[t])
        enc_buf[h, pl.ds(t * TILE, TILE), :] = attend(
            mesh_q[t * TILE : (t + 1) * TILE], key, value, mask
        )
        chain_start(*enc_items[t])
    pass_out(H - 1)
    if gathers:
        for k in (1, 2):
            for item in out_items(k):
                gather_start(*item)
        gather_wait(1, b_view)
    for s in range(1, H):
        for item in enc_items:
            chain_step(*item, s)
    if gathers:
        for item in out_items(0):
            gather_wait(*item[:2])

    mesh_one = (
        mesh_full + dot(lanes_of(enc_buf, everything), o_buf[0])
    ).astype(BF16)
    made = dot(normalize(mesh_one.astype(F32)), b_buf[:, 0 : 3 * cols])
    window_q = (made[:, :cols] * scaling).astype(BF16)
    wkv[pl.ds(mesh_rows, mesh_rows), :] = made[:, cols:].astype(BF16)
    own = wkv.at[pl.ds(mesh_rows, mesh_rows), :]
    window_halo = [
        (0, rim_parts, own, wkv.at[pl.ds(2 * mesh_rows, mesh_rows), :]),
        (1, rim_parts, own, wkv.at[pl.ds(0, mesh_rows), :]),
    ]
    for args in window_halo:
        start_halo(args)
    if gathers:
        for item in out_items(1):
            gather_pass(*item[:2])
    for args in window_halo:
        wait_halo(args)
    width = wo.shape[1]
    for t in range(mesh_tiles):
        key, value = blocks_of(wkv, t, 2 * mesh_tiles + 1)
        place = place_of(2 * mesh_tiles + 1)
        reached = n * mesh_tiles + t - mesh_tiles + place
        chosen = live_slots(place, [mesh_tiles + wo[t, s] for s in range(width)], width)
        mask = chosen & (reached >= 0) & (reached < mesh_tiles * N)
        win_buf[h, pl.ds(t * TILE, TILE), :] = attend(
            window_q[t * TILE : (t + 1) * TILE], key, value, mask
        )
        chain_start(*win_items[t])
    for s in range(1, H):
        for item in win_items:
            chain_step(*item, s)
    if gathers:
        for item in out_items(1):
            gather_wait(*item[:2])
    mesh_two = (
        mesh_one.astype(F32) + dot(lanes_of(win_buf, everything), o_buf[1])
    ).astype(BF16)
    for i in range(H):
        two_buf[i] = mesh_two[:, i * part_features : (i + 1) * part_features]
    units = b_buf.shape[1] - 5 * cols
    first = 3 * cols
    hidden = dot(normalize(mesh_two.astype(F32)), b_buf[:, first : first + units])
    hidden = (0.5 * hidden * (1.0 + lax.erf(hidden * (0.5**0.5)))).astype(BF16)
    if gathers:
        gather_wait(2, s_view)

    def term(lane):
        mine = pl.ds(pl.multiple_of(lane * part_features, part_features), part_features)
        return dot(hidden, s_buf[:, mine])

    def part_copy(d, lane):
        return copy(rs_src.at[d], rs_dst.at[d], rs_s.at[d], rs_r.at[d], (n, lane))

    for d in range(1, H):
        lane = lax.rem(h + d, H)
        rs_src[d] = term(lane).astype(BF16)
        part_copy(d, lane).start()
    total = two_buf[h].astype(F32) + term(h)
    for d in range(1, H):
        part_copy(d, lax.rem(h + d, H)).wait_recv()
        total = total + rs_dst[d].astype(F32)
    three = total.astype(BF16)
    three_buf[h] = three
    chain_start(THREE_ITEM, whole(three_buf))
    mesh_out[...] = three
    if gathers:
        for item in out_items(2):
            gather_pass(*item[:2])
    for s in range(1, H):
        chain_step(THREE_ITEM, whole(three_buf), s)
    mesh_norm = normalize(lanes_of(three_buf, everything).astype(F32))
    made = dot(mesh_norm, b_buf[:, first + units :])
    dkv[pl.ds(TILE, mesh_rows), :] = made.astype(BF16)
    decoder_halo = [
        (0, rim_parts + 1, dkv.at[pl.ds(TILE, TILE), :], dkv.at[pl.ds(TILE + mesh_rows, TILE), :]),
        (1, rim_parts + 1, dkv.at[pl.ds(mesh_rows, TILE), :], dkv.at[pl.ds(0, TILE), :]),
    ]
    for args in decoder_halo:
        start_halo(args)
    for args in decoder_halo:
        wait_halo(args)
    base_mesh = n * mesh_tiles - 1
    width = db.shape[0]
    place = place_of(mesh_tiles + 2)
    key, value = blocks_of(dkv, 0, mesh_tiles + 2)
    per_part = grid_tiles // PARTS
    for c in range(PARTS):
        for u in range(per_part):
            g = c * per_part + u
            mask = live_slots(place, [db[s, g] - base_mesh for s in range(width)], dc[g])
            rows = pl.ds(g * TILE, TILE)
            dec_buf[h, rows, :] = attend(gq[rows, :], key, value, mask)
        chain_start(DEC_ITEM + c, dec_view(c))
        if c > 0:
            chain_step(DEC_ITEM + c - 1, dec_view(c - 1), 1)
    chain_step(DEC_ITEM + PARTS - 1, dec_view(PARTS - 1), 1)
    mine = pl.ds(pl.multiple_of(h * part_features, part_features), part_features)
    if gathers:
        for item in out_items(2):
            gather_wait(*item[:2])
    dec_weight = o_buf[2, :, mine]
    for s in range(2, H - 1):
        for c in range(PARTS):
            chain_step(DEC_ITEM + c, dec_view(c), s)
    for c in range(PARTS):
        chain_step(DEC_ITEM + c, dec_view(c), H - 1)
        rows = pl.ds(c * chunk, chunk)
        update = dot(lanes_of(dec_buf, rows), dec_weight)
        grid_out[rows, :] = (grid_buf[h, rows, :].astype(F32) + update).astype(BF16)

    for c in range(PARTS):
        chain_drain(c, grid_view(c))
        chain_drain(DEC_ITEM + c, dec_view(c))
        drain_halo(halo_enc(c))
    chain_drain(MESH_ITEM, whole(mesh_buf))
    for item in enc_items + win_items:
        chain_drain(*item)
    chain_drain(THREE_ITEM, whole(three_buf))
    for args in window_halo + decoder_halo:
        drain_halo(args)
    for d in range(1, H):
        part_copy(d, lax.rem(h + d, H)).wait_send()
    if gathers:
        for k in range(3):
            chain_drain(OUT_ITEM + k, o_chain(k))
            for item in out_items(k):
                gather_drain(*item[:2])
        gather_drain(0, a_view)
        gather_drain(1, b_view)
        gather_drain(2, s_view)


def local(
    grid_state, mesh_state,
    encoder_query, encoder_key, encoder_value, encoder_output,
    window_query, window_key, window_value, window_output,
    expand_weight, shrink_weight,
    decoder_query, decoder_key, decoder_value, decoder_output,
    encoder_blocks, encoder_count, window_offsets, decoder_blocks, decoder_count,
):
    N, H = lax.axis_size("nodes"), lax.axis_size("heads")
    grid_rows, part = grid_state.shape
    mesh_rows = mesh_state.shape[0]
    shard, cols = encoder_key.shape
    features = part * H
    gathers = N % 2 == 0 and shard % 128 == 0
    V = pltpu.VMEM
    DMA = pltpu.SemaphoreType.DMA
    units = expand_weight.shape[1]
    if gathers:
        weights = (
            encoder_query, encoder_key, encoder_value, encoder_output,
            window_query, window_key, window_value, window_output,
            expand_weight, shrink_weight,
            decoder_query, decoder_key, decoder_value, decoder_output,
        )
        scratch = [
            V((features, 4 * cols), BF16),
            V((features, 5 * cols + units), BF16),
            V((units, features), BF16),
            V((3, H, cols, shard), BF16),
            V((3, H * cols, features), BF16),
        ]
    else:
        a = jnp.concatenate([encoder_key, encoder_value, decoder_query, encoder_query], axis=1)
        b = jnp.concatenate(
            [
                window_query, window_key, window_value, expand_weight,
                decoder_key, decoder_value,
            ],
            axis=1,
        )
        out = jnp.stack([encoder_output, window_output, decoder_output])
        weights = (
            lax.all_gather(a, "nodes", axis=0, tiled=True),
            lax.all_gather(b, "nodes", axis=0, tiled=True),
            lax.all_gather(shrink_weight, "nodes", axis=1, tiled=True),
            lax.all_gather(
                lax.all_gather(out, "nodes", axis=2, tiled=True), "heads", axis=1, tiled=True
            ),
        )
        scratch = []
    scratch += [DMA((16,))]
    items = 2 * PARTS + 7 + 2 * (mesh_rows // TILE)
    scratch += [
        V((H, grid_rows, part), BF16),
        V((2 * grid_rows, 2 * cols), BF16),
        V((grid_rows, cols), BF16),
        V((H, mesh_rows, part), BF16),
        V((H, mesh_rows, cols), BF16),
        V((H, mesh_rows, cols), BF16),
        V((H, mesh_rows, part), BF16),
        V((3 * mesh_rows, 2 * cols), BF16),
        V((H, mesh_rows, part), BF16),
        V((H, mesh_rows, part), BF16),
        V((H, mesh_rows, part), BF16),
        V((mesh_rows + 2 * TILE, 2 * cols), BF16),
        V((H, grid_rows, cols), BF16),
        DMA((2, items, H)),
        DMA((items, H)),
        DMA((2, PARTS // 2 + 2)),
        DMA((2, PARTS // 2 + 2)),
        DMA((H,)),
        DMA((H,)),
    ]
    if gathers:
        scratch += [DMA((3 + 3 * H, N // 2)), DMA((3 + 3 * H, N)), DMA((3 + 3 * H, N))]
    smem = pl.BlockSpec(memory_space=pltpu.SMEM)
    vmem = pl.BlockSpec(memory_space=pltpu.VMEM)
    hbm = pl.BlockSpec(memory_space=pl.ANY)
    kept = [hbm] * len(weights) if gathers else [vmem] * len(weights)
    return pl.pallas_call(
        functools.partial(kernel, N, H, gathers),
        out_shape=(
            jax.ShapeDtypeStruct(grid_state.shape, BF16),
            jax.ShapeDtypeStruct(mesh_state.shape, BF16),
        ),
        in_specs=[smem] * 5 + [hbm] * 2 + kept,
        out_specs=(vmem, vmem),
        scratch_shapes=scratch,
        compiler_params=pltpu.CompilerParams(
            collective_id=0, has_side_effects=True
        ),
    )(
        encoder_blocks, encoder_count, window_offsets, decoder_blocks.T, decoder_count,
        grid_state, mesh_state, *weights,
    )


def solution(mesh):
    rows, columns = P("nodes", "heads"), P("heads", "nodes")
    in_specs = (
        (rows,) * 5 + (columns,) + (rows,) * 3 + (columns,) + (rows, columns)
        + (rows,) * 3 + (columns,)
        + (P("nodes", None), P("nodes"), P("nodes", None), P("nodes", None), P("nodes"))
    )
    return jax.shard_map(
        local, mesh=mesh, in_specs=in_specs, out_specs=(rows, rows), check_vma=False
    )
```
